32 devices in a mesh: region: 2 (over y), member: 8 (over z, core), space: 2 (over x).
Axes of the slice: x: 2, y: 2, z: 4, core: 2. Of those that a mesh axis runs over, the one named last changes fastest.
Arguments:
- prior_trials: bfloat16 [80, 1536, 256], P('member', ('region', 'space')), parts along dimension 1, may hold values from -6 to 6
- prior_at_sensors: bfloat16 [80, 1536], P('member', ('region', 'space')), parts along dimension 1, may hold values from -6 to 6
- sensor_readings: bfloat16 [1536], P(('region', 'space')), parts along dimension 0, may hold values from -8 to 8
- sensor_noise_spread: bfloat16 [1536], P(('region', 'space')), parts along dimension 0, may hold values from 1 to 10
- nearby_readings: int32 [1536, 128], P(('region', 'space')), parts along dimension 0, may hold values from 0 to 1023, as said below
- subarea_cutoff_level: int32 [1536], P(('region', 'space')), parts along dimension 0, may hold values from 0 to 3
Outputs:
- analysis: bfloat16 [80, 1536, 256], P('member', ('region', 'space')), parts along dimension 1
The draws below stay inside these ranges and needn't reach their ends.
There are 2 independent parts, one for each index of `region`. The reference program is written for one: setup_inputs(seed, part) draws one part's arguments, and reference() takes and returns one part's arrays. A program takes and returns all parts, laid end to end along the dimension named above; each array names one. Nothing has to cross between parts.
Inputs may be any that keep to these rules, and one draw needn't show every extreme that they name: `nearby_readings`: row c lists 128 distinct observations whose region-wide index o lies within (subarea_cutoff_level[c] + 2) * 64 of c and inside the region.
All inputs are finite; a program needn't handle non-finite values. Where the reference program divides by a largest or mean magnitude, that divisor is 1e-20 or more.
Results may differ from the reference program's by a relative error of at most 0.0053.
Values may be sent and summed in bfloat16 or wider, within the bound.
A program may use at most 64 MiB of HBM per device.

```python
import math
import jax
import jax.numpy as jnp
from jax import lax

TRIAL_COUNT = 80
CELL_QUANTITIES = 256
OBS_DOM = 128
TIERS = 4
NS_STEPS = 4
PATCH_CELLS = 384
AREA_CELLS = 768
HALO = 320


def tier_table(key):
    return jax.random.randint(jax.random.fold_in(key, 11), (AREA_CELLS,), 0, TIERS).astype(jnp.int32)


def draw_subarea_cutoff_level(key, part):
    return tier_table(key)


def draw_nearby_readings(key, part):
    tier_ids = tier_table(key)
    columns = jnp.arange(AREA_CELLS, dtype=jnp.int32)
    width_all = 2 * HALO + 1
    offsets = jnp.arange(width_all, dtype=jnp.int32) - HALO
    reach_twice = (tier_ids + 2) * OBS_DOM
    position = columns[:, None] + offsets[None, :]
    usable = (2 * jnp.abs(offsets)[None, :] <= reach_twice[:, None]) & (position >= 0) & (position < AREA_CELLS)
    raw_bits = jax.random.randint(jax.random.fold_in(key, 12), (AREA_CELLS, width_all), 0, 1 << 20).astype(jnp.int32)
    slot_ids = (offsets + HALO)[None, :]
    score = jnp.where(usable, raw_bits * width_all + slot_ids, -1 - slot_ids)
    unused, chosen = lax.top_k(score, OBS_DOM)
    return ((columns % PATCH_CELLS)[:, None] + chosen).astype(jnp.int32)


def draw_sensor_readings(key, part):
    ramp = jnp.arange(AREA_CELLS, dtype=jnp.float32) / AREA_CELLS
    noise = jnp.clip(jax.random.normal(jax.random.fold_in(key, 22), (AREA_CELLS,), jnp.float32), -4.0, 4.0)
    values = 0.6 * (1.0 + 2.0 * ramp) * noise
    return values.astype(jnp.bfloat16)


def block_levels(key, extent, split, low, largest):
    level, own = 1.0, jax.random.fold_in(key, 6)
    for dim, parts in split:
        heights = jnp.exp(jax.random.uniform(jax.random.fold_in(own, dim), (parts,), jnp.float32, low / len(split), largest / len(split)))
        level = level * jnp.repeat(heights, extent[dim] // parts).reshape([-1 if axis == dim else 1 for axis in range(len(extent))])
    return level


def gaussian(own_key, shape, scale, most, pieces=(), kind=jnp.bfloat16):
    drawn = scale * jax.random.normal(own_key, shape, jnp.float32)
    if pieces:
        drawn = drawn * block_levels(own_key, shape, pieces, -0.22, 0.18)
    return jnp.clip(drawn, -most, most).astype(kind)


def setup_inputs(seed: int = 0, part: int = 0) -> dict:
    keys = jax.random.split(jax.random.key(seed), 7)
    own_keys = jax.random.split(jax.random.fold_in(keys[6], part), 7)
    return {
        "prior_trials": gaussian(own_keys[0], (TRIAL_COUNT, AREA_CELLS, CELL_QUANTITIES), 1.0, 6.0, ((0, 8), (1, 2))),
        "prior_at_sensors": gaussian(own_keys[1], (TRIAL_COUNT, AREA_CELLS), 1.0, 6.0, ((0, 8), (1, 2))),
        "sensor_readings": draw_sensor_readings(jax.random.fold_in(jax.random.fold_in(keys[6], part), 71), part),
        "sensor_noise_spread": jnp.clip(jnp.exp(math.log(10.0) - 2.3025851 * jax.random.uniform(own_keys[3], (AREA_CELLS,), jnp.float32) ** block_levels(own_keys[3], (AREA_CELLS,), ((0, 2),), -0.2, 0.2)), 1.0, 10.0).astype(jnp.bfloat16),
        "nearby_readings": draw_nearby_readings(jax.random.fold_in(jax.random.fold_in(keys[6], part), 71), part),
        "subarea_cutoff_level": draw_subarea_cutoff_level(jax.random.fold_in(jax.random.fold_in(keys[6], part), 71), part),
    }


def prepare(picked, trial_lines, offsets, tier_ids, obs_count):
    observ = picked[:trial_lines]
    ens_mean = lax.optimization_barrier(jnp.mean(observ, axis=0))
    anomaly = observ - ens_mean
    innovation = picked[trial_lines] - ens_mean
    radius = (tier_ids.astype(jnp.float32) + 2.0) * (0.5 * obs_count)
    distance = jnp.abs(offsets).astype(jnp.float32) / radius[:, None]
    weight = jnp.exp(-2.0 * distance * distance) / picked[trial_lines + 1]
    return (anomaly, innovation, weight)

def spread_terms(anomaly, innovation, weight, trial_lines):
    fit_sum = jnp.sum(weight * innovation * innovation)
    spread = jnp.sum(weight * lax.optimization_barrier(jnp.sum(anomaly * anomaly, axis=0))) / (trial_lines - 1.0)
    return (fit_sum, spread)

def transform(anomaly, innovation, weight, inflation, trial_lines, sweeps):
    exact = lax.Precision.HIGHEST
    weighted = anomaly * weight[None]
    gram = jnp.einsum('ank,bnk->abn', weighted, anomaly, precision=exact)
    identity = jnp.eye(trial_lines, dtype=jnp.float32)[:, :, None]
    matrix = gram + (trial_lines - 1.0) / inflation * identity
    row_bound = lax.optimization_barrier(jnp.max(lax.optimization_barrier(jnp.sum(jnp.abs(matrix), axis=1)), axis=0))
    root_iter = matrix / row_bound
    inverse = jnp.broadcast_to(identity, matrix.shape)
    for repeat in range(sweeps):
        factor = 1.5 * identity - 0.5 * jnp.einsum('abn,bcn->acn', inverse, root_iter, precision=exact)
        root_iter = jnp.einsum('abn,bcn->acn', root_iter, factor, precision=exact)
        inverse = jnp.einsum('abn,bcn->acn', factor, inverse, precision=exact)
    inv_root = inverse / jnp.sqrt(row_bound)
    target = lax.optimization_barrier(jnp.sum(weighted * innovation[None], axis=2))
    half_gain = jnp.einsum('abn,bn->an', inv_root, target, precision=exact)
    mean_gain = jnp.einsum('abn,bn->an', inv_root, half_gain, precision=exact)
    weights_full = jnp.sqrt(trial_lines - 1.0) * inv_root + mean_gain[:, None, :]
    centred = weights_full - lax.optimization_barrier(jnp.mean(weights_full, axis=0, keepdims=True)) + 1.0 / trial_lines
    return centred.astype(jnp.bfloat16)

def reference(prior_trials, prior_at_sensors, sensor_readings, sensor_noise_spread, nearby_readings, subarea_cutoff_level):
    trial_lines = prior_at_sensors.shape[0]
    obs_count = nearby_readings.shape[1]
    columns = jnp.arange(AREA_CELLS, dtype=jnp.int32)
    global_obs = (nearby_readings + (columns // PATCH_CELLS * PATCH_CELLS - HALO)[:, None]).astype(jnp.int32)
    block_count = AREA_CELLS // PATCH_CELLS

    def block_data(block_no):
        patch_start_index = (block_no * PATCH_CELLS).astype(jnp.int32)
        obs_lists = lax.dynamic_slice_in_dim(global_obs, patch_start_index, PATCH_CELLS, 0)
        col_ids = lax.dynamic_slice_in_dim(columns, patch_start_index, PATCH_CELLS, 0)
        tier_ids = lax.dynamic_slice_in_dim(subarea_cutoff_level, patch_start_index, PATCH_CELLS, 0)
        ens_part = jnp.take(prior_at_sensors, obs_lists, axis=1).astype(jnp.float32)
        value_part = jnp.take(sensor_readings, obs_lists).astype(jnp.float32)[None]
        error_part = jnp.take(sensor_noise_spread, obs_lists).astype(jnp.float32)[None]
        picked = jnp.concatenate([ens_part, value_part, error_part], axis=0)
        return prepare(picked, trial_lines, obs_lists - col_ids[:, None], tier_ids, obs_count)

    def block_sums(block_no):
        anomaly, innovation, weight = block_data(block_no)
        return spread_terms(anomaly, innovation, weight, trial_lines)
    fits, spreads = lax.map(block_sums, jnp.arange(block_count, dtype=jnp.int32))
    inflation = jnp.sum(fits) / jnp.sum(spreads)

    def block_analysis(block_no):
        anomaly, innovation, weight = block_data(block_no)
        trans_w = transform(anomaly, innovation, weight, inflation, trial_lines, NS_STEPS)
        trans_w = lax.optimization_barrier(trans_w).astype(jnp.float32)
        patch_start_index = (block_no * PATCH_CELLS).astype(jnp.int32)
        quantity_lines = lax.dynamic_slice_in_dim(prior_trials, patch_start_index, PATCH_CELLS, 1).astype(jnp.float32)
        updated = jnp.einsum('inc,ijn->jnc', quantity_lines, trans_w, precision=lax.Precision.HIGHEST)
        return updated.astype(jnp.bfloat16)
    piled_pieces = lax.map(block_analysis, jnp.arange(block_count, dtype=jnp.int32))
    return jnp.transpose(piled_pieces, (1, 0, 2, 3)).reshape(trial_lines, AREA_CELLS, prior_trials.shape[2])
```

```python
import functools

import jax
import jax.numpy as jnp
from jax import lax
from jax.experimental import pallas as pl
from jax.experimental.pallas import tpu as pltpu
from jax.sharding import PartitionSpec as P

NS_STEPS = 4
LANES = 128
GROUP = 4
MESH = pl.DeviceIdType.MESH
F32 = jnp.float32
BF16 = jnp.bfloat16


def partner(me, k, n):
    if n & (n - 1):
        return lax.rem(me + k, n)
    other, bit = me, 1
    while bit < n:
        if k & bit:
            other = other + bit * (1 - 2 * lax.rem(me // bit, 2))
        bit *= 2
    return other


def split(value):
    high = value.astype(BF16)
    return high, (value - high.astype(F32)).astype(BF16)


def times(left, right):
    lh, ll = split(left)
    rh, rl = split(right)
    rows, k = left.shape[0], right.shape[0]
    lhs = jnp.concatenate([lh, ll], axis=0)[:, :k]
    rhs = jnp.concatenate([rh, rl], axis=1)
    out = jnp.dot(lhs, rhs, preferred_element_type=F32)
    width = right.shape[1]
    return out[:rows, :width] + out[:rows, width:] + out[rows:, :width]


def analyse_kernel(
    n, spaces, halo, obs_count, x, pack, lists, radius,
    incoming, trans_out,
    gathered, full, anoms, anoms_t, marks, weights, gram, target, moved, sums, sums2,
    bulk_send, bulk_recv, local_sem, side_send, side_recv, sum_send, sum_recv, sum2_send, sum2_recv,
):
    me = lax.axis_index("member")
    space = lax.axis_index("space")
    members, patch, _ = x.shape
    domains = patch // n
    lines = members * n
    width = anoms.shape[1]

    barrier = pltpu.get_barrier_semaphore()

    def greet(k, carry):
        other = lax.rem(me + space * n + k, n * spaces)
        pl.semaphore_signal(
            barrier, inc=1,
            device_id={"member": lax.rem(other, n), "space": other // n},
            device_id_type=MESH,
        )
        return carry

    lax.fori_loop(1, n * spaces, greet, 0)
    pl.semaphore_wait(barrier, n * spaces - 1)

    def side_copy(side, k):
        to_space = lax.rem(space + 1 - side + spaces, spaces)
        to = partner(me, k, n)
        return pltpu.make_async_remote_copy(
            pack, gathered.at[side, me], side_send.at[side, k], side_recv.at[side, k],
            device_id={"member": to, "space": to_space}, device_id_type=MESH,
        )

    has_left, has_right = space > 0, space < spaces - 1
    for k in range(1, n):
        side_copy(1, k).start()

    @pl.when(has_right)
    def _():
        for k in range(n):
            side_copy(0, k).start()

    @pl.when(has_left)
    def _():
        for k in range(n):
            side_copy(2, k).start()

    bulk = []
    for k in range(1, n):
        to = partner(me, k, n)
        copy = pltpu.make_async_remote_copy(
            x.at[:, pl.ds(pl.multiple_of(to * domains, 16), domains), :],
            incoming.at[pl.ds(me * members, members)],
            bulk_send.at[k], bulk_recv.at[k],
            device_id={"member": to}, device_id_type=MESH,
        )
        copy.start()
        bulk.append(copy)
    own = pltpu.make_async_copy(
        x.at[:, pl.ds(pl.multiple_of(me * domains, 16), domains), :],
        incoming.at[pl.ds(me * members, members)], local_sem,
    )
    own.start()

    gathered[1, me] = pack[...]

    @pl.when(space == 0)
    def _():
        gathered[0] = jnp.ones(gathered.shape[1:], BF16)

    @pl.when(space == spaces - 1)
    def _():
        gathered[2] = jnp.ones(gathered.shape[1:], BF16)

    lane = lax.broadcasted_iota(jnp.int32, (obs_count, width), 1)

    def mark(group, carry):
        start = pl.multiple_of(group * 8, 8)
        columns = jnp.transpose(lists[pl.ds(start, 8), :] - me * domains)
        rows = []
        for d in range(8):
            hit = columns[:, d : d + 1] == lane
            rows.append(jnp.sum(jnp.where(hit, 1.0, 0.0), axis=0, keepdims=True))
        marks[pl.ds(start, 8), :] = jnp.concatenate(rows, axis=0)
        return carry

    lax.fori_loop(0, domains // 8, mark, 0)

    for k in range(1, n):
        side_copy(1, k).wait()

    @pl.when(has_right)
    def _():
        for k in range(n):
            side_copy(0, k).wait_send()
            side_copy(2, k).wait_recv()

    @pl.when(has_left)
    def _():
        for k in range(n):
            side_copy(2, k).wait_send()
            side_copy(0, k).wait_recv()

    for side in range(3):
        for s in range(n):
            full[members * s : members * (s + 1), patch * side : patch * (side + 1)] = (
                gathered[side, s, :members, :].astype(F32)
            )
        full[lines : lines + 2, patch * side : patch * (side + 1)] = (
            gathered[side, 0, members : members + 2, :].astype(F32)
        )
    total = 3 * patch
    shift = lax.rem(2 * total - (patch - halo) - me * domains, total)
    turned = pltpu.roll(full[...], shift, 1)[:, :width]
    values = turned[:lines]
    mean = jnp.sum(values, axis=0, keepdims=True) * (1.0 / lines)
    anomaly = values - mean
    anoms[...] = anomaly
    innov = turned[lines : lines + 1] - mean
    noise = turned[lines + 1 : lines + 2]
    squares = jnp.sum(anomaly * anomaly, axis=0, keepdims=True)

    place = lax.broadcasted_iota(jnp.int32, (domains, width), 1)
    row = lax.broadcasted_iota(jnp.int32, (domains, width), 0)
    distance = jnp.abs(place - halo - row).astype(F32) / radius[...]
    weight = marks[...] * jnp.exp(-2.0 * distance * distance) / noise
    weights[...] = weight
    fit = jnp.sum(weight * (innov * innov))
    spread = jnp.sum(weight * squares)
    first = lax.broadcasted_iota(jnp.int32, (8, LANES), 0) == 0
    moved[0] = jnp.where(first, fit, spread)

    high, low = split(anomaly)
    pad = jnp.zeros((LANES - lines, width), F32)
    anoms_t[...] = jnp.concatenate(
        [
            jnp.transpose(jnp.concatenate([high.astype(F32), pad], axis=0)),
            jnp.transpose(jnp.concatenate([low.astype(F32), pad], axis=0)),
        ],
        axis=1,
    ).astype(BF16)

    sum_copies = []
    for k in range(1, n):
        copy = pltpu.make_async_remote_copy(
            moved.at[0], sums.at[k], sum_send.at[k], sum_recv.at[k],
            device_id={"member": partner(me, k, n) if not n & (n - 1) else lax.rem(me + n - k, n)},
            device_id_type=MESH,
        )
        copy.start()
        sum_copies.append(copy)

    def one_gram(c):
        weighted = anoms[...] * weights[pl.ds(c, 1), :]
        hi, lo = split(weighted)
        out = jnp.dot(
            jnp.concatenate([hi, lo], axis=0), anoms_t[...], preferred_element_type=F32
        )
        gram[c] = out[:lines, :LANES] + out[:lines, LANES:] + out[lines:, :LANES]
        aim = jnp.sum(weighted * innov, axis=1, keepdims=True)
        target[c] = jnp.broadcast_to(aim, (lines, LANES))

    def gram_group(g, carry):
        for d in range(2):
            one_gram(g * 2 + d)
        return carry

    half = domains // 4
    lax.fori_loop(0, half, gram_group, 0)

    for copy in sum_copies:
        copy.wait()
    partial = moved[0]
    for k in range(1, n):
        partial = partial + sums[k]
    moved[1] = partial
    sum2_copies = []
    for k in range(1, spaces):
        copy = pltpu.make_async_remote_copy(
            moved.at[1], sums2.at[k], sum2_send.at[k], sum2_recv.at[k],
            device_id={"space": lax.rem(space + k, spaces)}, device_id_type=MESH,
        )
        sum2_copies.append(copy)
    gram_group(half, 0)
    for copy in sum2_copies:
        copy.start()
    lax.fori_loop(half + 1, domains // 2, gram_group, 0)
    for copy in sum2_copies:
        copy.wait()
    for k in range(1, spaces):
        partial = partial + sums2[k]
    scale = (lines - 1.0) * (partial[1:2, :] / (lines - 1.0)) / partial[0:1, :]

    eye = jnp.where(
        lax.broadcasted_iota(jnp.int32, (lines, LANES), 0)
        == lax.broadcasted_iota(jnp.int32, (lines, LANES), 1),
        1.0, 0.0,
    )
    diagonal = eye * scale

    def solve_group(g, carry):
        ids = [g * GROUP + d for d in range(GROUP)]
        mats = [gram[c] + diagonal for c in ids]
        bounds = [
            jnp.max(jnp.sum(jnp.abs(m), axis=0, keepdims=True), axis=1, keepdims=True)
            for m in mats
        ]
        ys = [m / b for m, b in zip(mats, bounds)]
        zs = [1.5 * eye - 0.5 * y for y in ys]
        ys = [times(y, z) for y, z in zip(ys, zs)]
        for step in range(1, NS_STEPS):
            ps = [1.5 * eye - 0.5 * times(z, y) for z, y in zip(zs, ys)]
            if step < NS_STEPS - 1:
                both = [
                    times(jnp.concatenate([y, z], axis=0), p) for y, z, p in zip(ys, zs, ps)
                ]
                ys = [b[:lines] for b in both]
                zs = [b[lines:] for b in both]
            else:
                zs = [times(z, p) for z, p in zip(zs, ps)]
        roots = [z * lax.rsqrt(b) for z, b in zip(zs, bounds)]
        for c, root in zip(ids, roots):
            half_gain = jnp.sum(root * target[c], axis=0, keepdims=True)
            gain = jnp.sum(root * half_gain, axis=1, keepdims=True)
            w = (lines - 1.0) ** 0.5 * root + gain
            w = w - jnp.sum(w, axis=0, keepdims=True) * (1.0 / lines) + 1.0 / lines
            trans_out[c] = w.astype(BF16)
        return carry

    lax.fori_loop(0, domains // GROUP, solve_group, 0)

    own.wait()
    for copy in bulk:
        copy.wait()


def spread_kernel(n, x, out, send, recv, local_sem):
    me = lax.axis_index("member")
    members, domains = x.shape[0] // n, x.shape[1]
    barrier = pltpu.get_barrier_semaphore()
    for k in range(1, n):
        pl.semaphore_signal(
            barrier, inc=1, device_id={"member": lax.rem(me + k, n)}, device_id_type=MESH
        )
    pl.semaphore_wait(barrier, n - 1)
    place = out.at[:, pl.ds(pl.multiple_of(me * domains, 16), domains), :]
    copies = []
    for k in range(1, n):
        to = partner(me, k, n)
        copy = pltpu.make_async_remote_copy(
            x.at[pl.ds(to * members, members)], place, send.at[k], recv.at[k],
            device_id={"member": to}, device_id_type=MESH,
        )
        copy.start()
        copies.append(copy)
    own = pltpu.make_async_copy(x.at[pl.ds(me * members, members)], place, local_sem)
    own.start()
    own.wait()
    for copy in copies:
        copy.wait()


def per_device(trials, sensors, readings, noise, lists, tiers):
    n, spaces = lax.axis_size("member"), lax.axis_size("space")
    members, patch, quantities = trials.shape
    obs_count = lists.shape[1]
    halo = 5 * obs_count // 2
    domains = patch // n
    lines = members * n
    width = -(-(domains + 2 * halo) // 256) * 256
    rows = -(-(members + 2) // 16) * 16
    first_col = lax.axis_index("member") * domains
    own_lists = lax.dynamic_slice_in_dim(lists, first_col, domains, 0)
    own_tiers = lax.dynamic_slice_in_dim(tiers, first_col, domains, 0)
    radius = ((own_tiers.astype(F32) + 2.0) * (0.5 * obs_count))[:, None]
    pack = jnp.concatenate(
        [sensors, readings[None], noise[None], jnp.ones((rows - members - 2, patch), BF16)], axis=0
    )
    vmem = pl.BlockSpec(memory_space=pltpu.VMEM)
    anywhere = pl.BlockSpec(memory_space=pl.ANY)
    full_rows = -(-(lines + 2) // 8) * 8
    dma = pltpu.SemaphoreType.DMA
    incoming, trans = pl.pallas_call(
        functools.partial(analyse_kernel, n, spaces, halo, obs_count),
        out_shape=(
            jax.ShapeDtypeStruct((lines, domains, quantities), BF16),
            jax.ShapeDtypeStruct((domains, lines, LANES), BF16),
        ),
        in_specs=[anywhere, vmem, vmem, vmem],
        out_specs=(anywhere, vmem),
        scratch_shapes=[
            pltpu.VMEM((3, n, rows, patch), BF16),
            pltpu.VMEM((full_rows, 3 * patch), F32),
            pltpu.VMEM((lines, width), F32),
            pltpu.VMEM((width, 2 * LANES), BF16),
            pltpu.VMEM((domains, width), F32),
            pltpu.VMEM((domains, width), F32),
            pltpu.VMEM((domains, lines, LANES), F32),
            pltpu.VMEM((domains, lines, LANES), F32),
            pltpu.VMEM((2, 8, LANES), F32),
            pltpu.VMEM((n, 8, LANES), F32),
            pltpu.VMEM((spaces, 8, LANES), F32),
            dma((n,)), dma((n,)), dma, dma((3, n)), dma((3, n)),
            dma((n,)), dma((n,)), dma((spaces,)), dma((spaces,)),
        ],
        compiler_params=pltpu.CompilerParams(
            collective_id=0, has_side_effects=True, vmem_limit_bytes=40 << 20
        ),
        name="analyse",
    )(trials, pack, own_lists, radius)
    updated = jnp.einsum(
        "inc,nij->jnc", incoming, trans[:, :, :lines], preferred_element_type=F32
    ).astype(BF16)
    return pl.pallas_call(
        functools.partial(spread_kernel, n),
        out_shape=jax.ShapeDtypeStruct((members, patch, quantities), BF16),
        in_specs=[vmem],
        out_specs=anywhere,
        scratch_shapes=[dma((n,)), dma((n,)), dma],
        compiler_params=pltpu.CompilerParams(collective_id=1, has_side_effects=True),
        name="spread",
    )(updated)


def solution(mesh):
    return jax.shard_map(
        per_device,
        mesh=mesh,
        in_specs=(
            P("member", ("region", "space"), None),
            P("member", ("region", "space")),
            P(("region", "space")),
            P(("region", "space")),
            P(("region", "space"), None),
            P(("region", "space")),
        ),
        out_specs=P("member", ("region", "space"), None),
        check_vma=False,
    )
```

```python
import functools

import jax
import jax.numpy as jnp
from jax import lax
from jax.experimental import pallas as pl
from jax.experimental.pallas import tpu as pltpu
from jax.sharding import PartitionSpec as P

NS_STEPS = 4
LANES = 128
GROUP = 4
CHUNK = 16
MESH = pl.DeviceIdType.MESH
F32 = jnp.float32
BF16 = jnp.bfloat16


def partner(me, k, n):
    if n & (n - 1):
        return lax.rem(me + k, n)
    other, bit = me, 1
    while bit < n:
        if k & bit:
            other = other + bit * (1 - 2 * lax.rem(me // bit, 2))
        bit *= 2
    return other


def split(value):
    high = value.astype(BF16)
    return high, (value - high.astype(F32)).astype(BF16)


def times(left, right):
    lh, ll = split(left)
    rh, rl = split(right)
    rows, k = left.shape[0], right.shape[0]
    lhs = jnp.concatenate([lh, ll], axis=0)[:, :k]
    rhs = jnp.concatenate([rh, rl], axis=1)
    out = jnp.dot(lhs, rhs, preferred_element_type=F32)
    width = right.shape[1]
    return out[:rows, :width] + out[:rows, width:] + out[rows:, :width]


def analyse_kernel(
    n, spaces, halo, obs_count, x, sensors, readings, noises, lists, tiers,
    out,
    pack, incoming, updated, gathered, full, anoms, anoms_t, marks, weights, gram, target, trans,
    moved, sums,
    in_send, in_recv, out_send, out_recv, local_sem, side_send, side_recv, sum_send, sum_recv,
):
    me = lax.axis_index("member")
    space = lax.axis_index("space")
    members, patch, _ = x.shape
    domains = patch // n
    lines = members * n
    width = anoms.shape[1]
    chunks = domains // CHUNK
    peers = n * spaces

    rows = pack.shape[0]
    pack[...] = jnp.concatenate(
        [
            sensors[...].astype(F32), readings[...].astype(F32), noises[...].astype(F32),
            jnp.ones((rows - members - 2, patch), F32),
        ],
        axis=0,
    ).astype(BF16)

    def peer(k):
        other = lax.rem(me + space * n + k, peers)
        return {"member": lax.rem(other, n), "space": other // n}

    barrier = pltpu.get_barrier_semaphore()

    def greet(k, carry):
        pl.semaphore_signal(barrier, inc=1, device_id=peer(k), device_id_type=MESH)
        return carry

    lax.fori_loop(1, peers, greet, 0)

    lane = lax.broadcasted_iota(jnp.int32, (obs_count, width), 1)

    def mark(group, carry):
        start = pl.multiple_of(group * 8, 8)
        source = pl.multiple_of(me * domains + group * 8, 8)
        columns = jnp.transpose(lists[pl.ds(source, 8), :] - me * domains)
        found = []
        for d in range(8):
            hit = columns[:, d : d + 1] == lane
            found.append(jnp.sum(jnp.where(hit, 1.0, 0.0), axis=0, keepdims=True))
        marks[pl.ds(start, 8), :] = jnp.concatenate(found, axis=0)
        return carry

    pl.semaphore_wait(barrier, peers - 1)

    def side_copy(side, k):
        to_space = lax.rem(space + 1 - side + spaces, spaces)
        return pltpu.make_async_remote_copy(
            pack, gathered.at[side, me], side_send.at[side, k], side_recv.at[side, k],
            device_id={"member": partner(me, k, n), "space": to_space}, device_id_type=MESH,
        )

    has_left, has_right = space > 0, space < spaces - 1
    for k in range(1, n):
        side_copy(1, k).start()

    @pl.when(has_right)
    def _():
        for k in range(n):
            side_copy(0, k).start()

    @pl.when(has_left)
    def _():
        for k in range(n):
            side_copy(2, k).start()

    def in_views(to, g):
        return (
            x.at[:, pl.ds(pl.multiple_of(to * domains + g * CHUNK, 16), CHUNK), :],
            incoming.at[pl.ds(me * members, members), pl.ds(g * CHUNK, CHUNK), :],
        )

    def in_copy(g, k):
        to = partner(me, k, n)
        source, place = in_views(to, g)
        return pltpu.make_async_remote_copy(
            source, place, in_send.at[g, k], in_recv.at[g, k],
            device_id={"member": to}, device_id_type=MESH,
        )

    far_first = list(range(n // 2, n)) + list(range(1, n // 2))
    pairs = [(g, k) for g in range(chunks) for k in far_first]
    early = n // 2 - 1
    for g, k in pairs[:early]:
        in_copy(g, k).start()
    own = []
    for g in range(chunks):
        source, place = in_views(me, g)
        copy = pltpu.make_async_copy(source, place, local_sem.at[0, g])
        copy.start()
        own.append(copy)

    gathered[1, me] = pack[...]

    @pl.when(space == 0)
    def _():
        gathered[0] = jnp.ones(gathered.shape[1:], BF16)

    @pl.when(space == spaces - 1)
    def _():
        gathered[2] = jnp.ones(gathered.shape[1:], BF16)

    lax.fori_loop(0, domains // 8, mark, 0)

    for k in range(1, n):
        side_copy(1, k).wait()

    @pl.when(has_right)
    def _():
        for k in range(n):
            side_copy(0, k).wait_send()
            side_copy(2, k).wait_recv()

    @pl.when(has_left)
    def _():
        for k in range(n):
            side_copy(2, k).wait_send()
            side_copy(0, k).wait_recv()

    for side in range(3):
        for s in range(n):
            full[members * s : members * (s + 1), patch * side : patch * (side + 1)] = (
                gathered[side, s, :members, :].astype(F32)
            )
        full[lines : lines + 2, patch * side : patch * (side + 1)] = (
            gathered[side, 0, members : members + 2, :].astype(F32)
        )
    total = 3 * patch
    shift = lax.rem(2 * total - (patch - halo) - me * domains, total)
    turned = pltpu.roll(full[...], shift, 1)[:, :width]
    values = turned[:lines]
    mean = jnp.sum(values, axis=0, keepdims=True) * (1.0 / lines)
    anomaly = values - mean
    anoms[...] = anomaly
    innov = turned[lines : lines + 1] - mean
    noise = turned[lines + 1 : lines + 2]
    squares = jnp.sum(anomaly * anomaly, axis=0, keepdims=True)

    own_tier = lax.broadcasted_iota(jnp.int32, (domains, patch), 1) == (
        lax.broadcasted_iota(jnp.int32, (domains, patch), 0) + me * domains
    )
    tier = jnp.sum(jnp.where(own_tier, tiers[...].astype(F32), 0.0), axis=1, keepdims=True)
    radius = (tier + 2.0) * (0.5 * obs_count)
    place = lax.broadcasted_iota(jnp.int32, (domains, width), 1)
    row = lax.broadcasted_iota(jnp.int32, (domains, width), 0)
    distance = jnp.abs(place - halo - row).astype(F32) / radius
    weight = marks[...] * jnp.exp(-2.0 * distance * distance) / noise
    weights[...] = weight
    fit = jnp.sum(weight * (innov * innov))
    spread = jnp.sum(weight * squares)
    first = lax.broadcasted_iota(jnp.int32, (8, LANES), 0) == 0
    moved[...] = jnp.where(first, fit, spread)

    high, low = split(anomaly)
    pad = jnp.zeros((LANES - lines, width), F32)
    anoms_t[...] = jnp.concatenate(
        [
            jnp.transpose(jnp.concatenate([high.astype(F32), pad], axis=0)),
            jnp.transpose(jnp.concatenate([low.astype(F32), pad], axis=0)),
        ],
        axis=1,
    ).astype(BF16)

    def sum_copy(k):
        return pltpu.make_async_remote_copy(
            moved, sums.at[k], sum_send.at[k], sum_recv.at[k],
            device_id=peer(k), device_id_type=MESH,
        )

    def start_sum(k, carry):
        sum_copy(k).start()
        return carry

    def end_sum(k, carry):
        sum_copy(k).wait()
        return carry + sums[k]

    lax.fori_loop(1, peers, start_sum, 0)
    for g, k in pairs[early:]:
        in_copy(g, k).start()

    hi, lo = split(weight * innov)
    aims = jnp.dot(jnp.concatenate([hi, lo], axis=0), anoms_t[...], preferred_element_type=F32)
    target[...] = aims[:domains, :LANES] + aims[:domains, LANES:] + aims[domains:, :LANES]

    def gram_group(g, carry):
        for d in range(2):
            c = g * 2 + d
            hi, lo = split(anoms[...] * weights[pl.ds(c, 1), :])
            prod = jnp.dot(
                jnp.concatenate([hi, lo], axis=0), anoms_t[...], preferred_element_type=F32
            )
            gram[c] = prod[:lines, :LANES] + prod[:lines, LANES:] + prod[lines:, :LANES]
        return carry

    lax.fori_loop(0, domains // 2, gram_group, 0)

    sums_all = lax.fori_loop(1, peers, end_sum, moved[...])
    scale = sums_all[1:2, :] / sums_all[0:1, :]
    eye = jnp.where(
        lax.broadcasted_iota(jnp.int32, (lines, LANES), 0)
        == lax.broadcasted_iota(jnp.int32, (lines, LANES), 1),
        1.0, 0.0,
    )
    diagonal = eye * scale

    def solve_group(g, carry):
        ids = [g * GROUP + d for d in range(GROUP)]
        mats = [gram[c] + diagonal for c in ids]
        bounds = [
            jnp.max(jnp.sum(jnp.abs(m), axis=0, keepdims=True), axis=1, keepdims=True)
            for m in mats
        ]
        ys = [m / b for m, b in zip(mats, bounds)]
        zs = [1.5 * eye - 0.5 * y for y in ys]
        ys = [times(y, z) for y, z in zip(ys, zs)]
        for step in range(1, NS_STEPS):
            ps = [1.5 * eye - 0.5 * times(z, y) for z, y in zip(zs, ys)]
            if step < NS_STEPS - 1:
                both = [
                    times(jnp.concatenate([y, z], axis=0), p) for y, z, p in zip(ys, zs, ps)
                ]
                ys = [b[:lines] for b in both]
                zs = [b[lines:] for b in both]
            else:
                zs = [times(z, p) for z, p in zip(zs, ps)]
        roots = [z * lax.rsqrt(b) for z, b in zip(zs, bounds)]
        for c, root in zip(ids, roots):
            half_gain = jnp.sum(root * target[pl.ds(c, 1), :], axis=1, keepdims=True)
            gain = jnp.sum(root * half_gain, axis=0, keepdims=True)
            w = (lines - 1.0) ** 0.5 * root + gain
            w = w - jnp.sum(w, axis=1, keepdims=True) * (1.0 / lines) + 1.0 / lines
            trans[c] = w.astype(BF16)
        return carry

    def out_views(to, g):
        return (
            updated.at[pl.ds(to * members, members), pl.ds(g * CHUNK, CHUNK), :],
            out.at[:, pl.ds(pl.multiple_of(me * domains + g * CHUNK, 16), CHUNK), :],
        )

    def out_copy(g, k):
        to = partner(me, k, n)
        source, place = out_views(to, g)
        return pltpu.make_async_remote_copy(
            source, place, out_send.at[g, k], out_recv.at[g, k],
            device_id={"member": to}, device_id_type=MESH,
        )

    for g in range(chunks):
        lax.fori_loop(g * CHUNK // GROUP, (g + 1) * CHUNK // GROUP, solve_group, 0)
        own[g].wait()
        for k in range(1, n):
            in_copy(g, k).wait()
        states = jnp.swapaxes(incoming[:, g * CHUNK : (g + 1) * CHUNK, :].astype(F32), 0, 1)
        states = states.astype(BF16)
        results = [
            jnp.dot(trans[g * CHUNK + c][:, :lines], states[c], preferred_element_type=F32)
            for c in range(CHUNK)
        ]
        results = jnp.stack(results, axis=0)
        updated[:, g * CHUNK : (g + 1) * CHUNK, :] = jnp.swapaxes(results, 0, 1).astype(BF16)
        for k in far_first:
            out_copy(g, k).start()
        source, place = out_views(me, g)
        copy = pltpu.make_async_copy(source, place, local_sem.at[1, g])
        copy.start()
        own.append(copy)

    for g in range(chunks):
        own[chunks + g].wait()
        for k in range(1, n):
            out_copy(g, k).wait()


def per_device(trials, sensors, readings, noises, lists, tiers):
    n, spaces = lax.axis_size("member"), lax.axis_size("space")
    members, patch, quantities = trials.shape
    obs_count = lists.shape[1]
    halo = 5 * obs_count // 2
    domains = patch // n
    chunks = domains // CHUNK
    lines = members * n
    width = -(-(domains + 2 * halo) // 256) * 256
    rows = -(-(members + 2) // 16) * 16
    vmem = pl.BlockSpec(memory_space=pltpu.VMEM)
    anywhere = pl.BlockSpec(memory_space=pl.ANY)
    full_rows = -(-(lines + 2) // 8) * 8
    dma = pltpu.SemaphoreType.DMA
    return pl.pallas_call(
        functools.partial(analyse_kernel, n, spaces, halo, obs_count),
        out_shape=jax.ShapeDtypeStruct((members, patch, quantities), BF16),
        in_specs=[anywhere] + [vmem] * 5,
        out_specs=vmem,
        scratch_shapes=[
            pltpu.VMEM((rows, patch), BF16),
            pltpu.VMEM((lines, domains, quantities), BF16),
            pltpu.VMEM((lines, domains, quantities), BF16),
            pltpu.VMEM((3, n, rows, patch), BF16),
            pltpu.VMEM((full_rows, 3 * patch), F32),
            pltpu.VMEM((lines, width), F32),
            pltpu.VMEM((width, 2 * LANES), BF16),
            pltpu.VMEM((domains, width), F32),
            pltpu.VMEM((domains, width), F32),
            pltpu.VMEM((domains, lines, LANES), F32),
            pltpu.VMEM((domains, LANES), F32),
            pltpu.VMEM((domains, lines, LANES), BF16),
            pltpu.VMEM((8, LANES), F32),
            pltpu.VMEM((n * spaces, 8, LANES), F32),
            dma((chunks, n)), dma((chunks, n)), dma((chunks, n)), dma((chunks, n)),
            dma((2, chunks)), dma((3, n)), dma((3, n)), dma((n * spaces,)), dma((n * spaces,)),
        ],
        compiler_params=pltpu.CompilerParams(
            collective_id=0, has_side_effects=True, vmem_limit_bytes=48 << 20
        ),
        name="analyse",
    )(trials, sensors, readings[None], noises[None], lists, tiers[None])


def solution(mesh):
    return jax.shard_map(
        per_device,
        mesh=mesh,
        in_specs=(
            P("member", ("region", "space"), None),
            P("member", ("region", "space")),
            P(("region", "space")),
            P(("region", "space")),
            P(("region", "space"), None),
            P(("region", "space")),
        ),
        out_specs=P("member", ("region", "space"), None),
        check_vma=False,
    )
```

```python
import functools

import jax
import jax.numpy as jnp
from jax import lax
from jax.experimental import pallas as pl
from jax.experimental.pallas import tpu as pltpu
from jax.sharding import PartitionSpec as P

NS_STEPS = 4
LANES = 128
GROUP = 4
CHUNK = 16
MESH = pl.DeviceIdType.MESH
F32 = jnp.float32
BF16 = jnp.bfloat16


def partner(me, k, n):
    if n & (n - 1):
        return lax.rem(me + k, n)
    other, bit = me, 1
    while bit < n:
        if k & bit:
            other = other + bit * (1 - 2 * lax.rem(me // bit, 2))
        bit *= 2
    return other


def split(value):
    high = value.astype(BF16)
    return high, (value - high.astype(F32)).astype(BF16)


def times(left, right):
    lh, ll = split(left)
    rh, rl = split(right)
    rows, k = left.shape[0], right.shape[0]
    lhs = jnp.concatenate([lh, ll], axis=0)[:, :k]
    rhs = jnp.concatenate([rh, rl], axis=1)
    out = jnp.dot(lhs, rhs, preferred_element_type=F32)
    width = right.shape[1]
    return out[:rows, :width] + out[:rows, width:] + out[rows:, :width]


def analyse_kernel(
    n, spaces, halo, obs_count, x, sensors_in, readings_in, noises_in, lists_in, tiers_in,
    out,
    sensors, readings, noises, lists, tiers, small_sem, pack, incoming, updated, gathered, full, anoms, anoms_t, marks, weights, gram, target, trans,
    moved, sums,
    in_send, in_recv, out_send, out_recv, local_sem, cross_send, cross_recv, side_send, side_recv, sum_send, sum_recv,
):
    me = lax.axis_index("member")
    space = lax.axis_index("space")
    members, patch, _ = x.shape
    domains = patch // n
    lines = members * n
    width = anoms.shape[1]
    chunks = domains // CHUNK
    peers = n * spaces

    small = [
        pltpu.make_async_copy(source, place, small_sem.at[i])
        for i, (source, place) in enumerate(
            [
                (sensors_in, sensors), (readings_in, readings), (noises_in, noises),
                (lists_in.at[pl.ds(pl.multiple_of(me * domains, 8), domains)], lists),
                (tiers_in, tiers),
            ]
        )
    ]
    for copy in small:
        copy.start()

    def peer(k):
        other = lax.rem(me + space * n + k, peers)
        return {"member": lax.rem(other, n), "space": other // n}

    barrier = pltpu.get_barrier_semaphore()

    def greet(k, carry):
        pl.semaphore_signal(barrier, inc=1, device_id=peer(k), device_id_type=MESH)
        return carry

    lax.fori_loop(1, peers, greet, 0)
    for copy in small:
        copy.wait()
    rows = pack.shape[0]
    pack[...] = jnp.concatenate(
        [
            sensors[...].astype(F32), readings[...].astype(F32)[None],
            noises[...].astype(F32)[None], jnp.ones((rows - members - 2, patch), F32),
        ],
        axis=0,
    ).astype(BF16)
    gathered[1, me] = pack[...]

    lane = lax.broadcasted_iota(jnp.int32, (obs_count, width), 1)

    def mark(group, carry):
        start = pl.multiple_of(group * 8, 8)
        columns = jnp.transpose(lists[pl.ds(start, 8), :] - me * domains)
        found = []
        for d in range(8):
            hit = columns[:, d : d + 1] == lane
            found.append(jnp.sum(jnp.where(hit, 1.0, 0.0), axis=0, keepdims=True))
        marks[pl.ds(start, 8), :] = jnp.concatenate(found, axis=0)
        return carry

    pl.semaphore_wait(barrier, peers - 1)

    def cross_copy(side):
        to_space = lax.rem(space + 1 - side + spaces, spaces)
        return pltpu.make_async_remote_copy(
            pack, gathered.at[side, me], cross_send.at[side], cross_recv.at[side],
            device_id={"space": to_space}, device_id_type=MESH,
        )

    def double_copies(side, step):
        stride = n >> (step + 1)
        to = partner(me, stride, n)
        held = 1 << step
        return [
            pltpu.make_async_remote_copy(
                gathered.at[side, lax.rem(me, 2 * stride) + j * 2 * stride],
                gathered.at[side, lax.rem(me, 2 * stride) + j * 2 * stride],
                side_send.at[side, held - 1 + j], side_recv.at[side, held - 1 + j],
                device_id={"member": to}, device_id_type=MESH,
            )
            for j in range(held)
        ]

    def each_side(act):
        act(1)

        @pl.when(has_left)
        def _():
            act(0)

        @pl.when(has_right)
        def _():
            act(2)

    def begin(step):
        return lambda side: [copy.start() for copy in double_copies(side, step)] and None

    def finish(step):
        return lambda side: [copy.wait() for copy in double_copies(side, step)] and None

    has_left, has_right = space > 0, space < spaces - 1

    @pl.when(has_right)
    def _():
        cross_copy(0).start()

    @pl.when(has_left)
    def _():
        cross_copy(2).start()

    def in_views(to, g):
        return (
            x.at[:, pl.ds(pl.multiple_of(to * domains + g * CHUNK, 16), CHUNK), :],
            incoming.at[pl.ds(me * members, members), pl.ds(g * CHUNK, CHUNK), :],
        )

    def in_copy(g, k):
        to = partner(me, k, n)
        source, place = in_views(to, g)
        return pltpu.make_async_remote_copy(
            source, place, in_send.at[g, k], in_recv.at[g, k],
            device_id={"member": to}, device_id_type=MESH,
        )

    far_first = list(range(n // 2, n)) + list(range(1, n // 2))
    pairs = [(g, k) for g in range(chunks) for k in far_first]
    early = n // 2 - 1
    for g, k in pairs[:early]:
        in_copy(g, k).start()
    own = []
    for g in range(chunks):
        source, place = in_views(me, g)
        copy = pltpu.make_async_copy(source, place, local_sem.at[0, g])
        copy.start()
        own.append(copy)

    @pl.when(has_right)
    def _():
        cross_copy(0).wait_send()
        cross_copy(2).wait_recv()

    @pl.when(has_left)
    def _():
        cross_copy(2).wait_send()
        cross_copy(0).wait_recv()

    each_side(begin(0))

    @pl.when(space == 0)
    def _():
        gathered[0] = jnp.ones(gathered.shape[1:], BF16)

    @pl.when(space == spaces - 1)
    def _():
        gathered[2] = jnp.ones(gathered.shape[1:], BF16)

    lax.fori_loop(0, domains // 8, mark, 0)

    for step in range(n.bit_length() - 1):
        if step:
            each_side(begin(step))
        each_side(finish(step))

    for side in range(3):
        for s in range(n):
            full[members * s : members * (s + 1), patch * side : patch * (side + 1)] = (
                gathered[side, s, :members, :].astype(F32)
            )
        full[lines : lines + 2, patch * side : patch * (side + 1)] = (
            gathered[side, 0, members : members + 2, :].astype(F32)
        )
    total = 3 * patch
    shift = lax.rem(2 * total - (patch - halo) - me * domains, total)
    turned = pltpu.roll(full[...], shift, 1)[:, :width]
    values = turned[:lines]
    mean = jnp.sum(values, axis=0, keepdims=True) * (1.0 / lines)
    anomaly = values - mean
    anoms[...] = anomaly
    innov = turned[lines : lines + 1] - mean
    noise = turned[lines + 1 : lines + 2]
    squares = jnp.sum(anomaly * anomaly, axis=0, keepdims=True)

    own_tier = lax.broadcasted_iota(jnp.int32, (domains, patch), 1) == (
        lax.broadcasted_iota(jnp.int32, (domains, patch), 0) + me * domains
    )
    tier = jnp.sum(jnp.where(own_tier, tiers[...].astype(F32)[None], 0.0), axis=1, keepdims=True)
    radius = (tier + 2.0) * (0.5 * obs_count)
    place = lax.broadcasted_iota(jnp.int32, (domains, width), 1)
    row = lax.broadcasted_iota(jnp.int32, (domains, width), 0)
    distance = jnp.abs(place - halo - row).astype(F32) / radius
    weight = marks[...] * jnp.exp(-2.0 * distance * distance) / noise
    weights[...] = weight
    fit = jnp.sum(weight * (innov * innov))
    spread = jnp.sum(weight * squares)
    first = lax.broadcasted_iota(jnp.int32, (1, LANES), 1) == 0
    moved[...] = jnp.where(first, fit, spread)

    high, low = split(anomaly)
    pad = jnp.zeros((LANES - lines, width), F32)
    anoms_t[...] = jnp.concatenate(
        [
            jnp.transpose(jnp.concatenate([high.astype(F32), pad], axis=0)),
            jnp.transpose(jnp.concatenate([low.astype(F32), pad], axis=0)),
        ],
        axis=1,
    ).astype(BF16)

    def sum_copy(k):
        return pltpu.make_async_remote_copy(
            moved, sums.at[k], sum_send.at[k], sum_recv.at[k],
            device_id=peer(k), device_id_type=MESH,
        )

    def start_sum(k, carry):
        sum_copy(k).start()
        return carry

    def end_sum(k, carry):
        sum_copy(k).wait()
        return carry + sums[k]

    lax.fori_loop(1, peers, start_sum, 0)
    for g, k in pairs[early:]:
        in_copy(g, k).start()

    hi, lo = split(weight * innov)
    aims = jnp.dot(jnp.concatenate([hi, lo], axis=0), anoms_t[...], preferred_element_type=F32)
    target[...] = aims[:domains, :LANES] + aims[:domains, LANES:] + aims[domains:, :LANES]

    def gram_group(g, carry):
        for d in range(2):
            c = g * 2 + d
            hi, lo = split(anoms[...] * weights[pl.ds(c, 1), :])
            prod = jnp.dot(
                jnp.concatenate([hi, lo], axis=0), anoms_t[...], preferred_element_type=F32
            )
            gram[c] = prod[:lines, :LANES] + prod[:lines, LANES:] + prod[lines:, :LANES]
        return carry

    lax.fori_loop(0, domains // 2, gram_group, 0)

    sums_all = lax.fori_loop(1, peers, end_sum, moved[...])
    scale = sums_all[:, 1:2] / sums_all[:, 0:1]
    eye = jnp.where(
        lax.broadcasted_iota(jnp.int32, (lines, LANES), 0)
        == lax.broadcasted_iota(jnp.int32, (lines, LANES), 1),
        1.0, 0.0,
    )
    diagonal = eye * scale

    def solve_group(g, carry):
        ids = [g * GROUP + d for d in range(GROUP)]
        mats = [gram[c] + diagonal for c in ids]
        bounds = [
            jnp.max(jnp.sum(jnp.abs(m), axis=0, keepdims=True), axis=1, keepdims=True)
            for m in mats
        ]
        ys = [m / b for m, b in zip(mats, bounds)]
        zs = [1.5 * eye - 0.5 * y for y in ys]
        ys = [times(y, z) for y, z in zip(ys, zs)]
        for step in range(1, NS_STEPS):
            ps = [1.5 * eye - 0.5 * times(z, y) for z, y in zip(zs, ys)]
            if step < NS_STEPS - 1:
                both = [
                    times(jnp.concatenate([y, z], axis=0), p) for y, z, p in zip(ys, zs, ps)
                ]
                ys = [b[:lines] for b in both]
                zs = [b[lines:] for b in both]
            else:
                zs = [times(z, p) for z, p in zip(zs, ps)]
        roots = [z * lax.rsqrt(b) for z, b in zip(zs, bounds)]
        for c, root in zip(ids, roots):
            half_gain = jnp.sum(root * target[pl.ds(c, 1), :], axis=1, keepdims=True)
            gain = jnp.sum(root * half_gain, axis=0, keepdims=True)
            w = (lines - 1.0) ** 0.5 * root + gain
            w = w - jnp.sum(w, axis=1, keepdims=True) * (1.0 / lines) + 1.0 / lines
            trans[c] = w.astype(BF16)
        return carry

    def out_views(to, g):
        return (
            updated.at[pl.ds(to * members, members), pl.ds(g * CHUNK, CHUNK), :],
            out.at[:, pl.ds(pl.multiple_of(me * domains + g * CHUNK, 16), CHUNK), :],
        )

    def out_copy(g, k):
        to = partner(me, k, n)
        source, place = out_views(to, g)
        return pltpu.make_async_remote_copy(
            source, place, out_send.at[g, k], out_recv.at[g, k],
            device_id={"member": to}, device_id_type=MESH,
        )

    for g in range(chunks):
        lax.fori_loop(g * CHUNK // GROUP, (g + 1) * CHUNK // GROUP, solve_group, 0)
        own[g].wait()
        for k in range(1, n):
            in_copy(g, k).wait()
        states = jnp.swapaxes(incoming[:, g * CHUNK : (g + 1) * CHUNK, :].astype(F32), 0, 1)
        states = states.astype(BF16)
        results = [
            jnp.dot(trans[g * CHUNK + c][:, :lines], states[c], preferred_element_type=F32)
            for c in range(CHUNK)
        ]
        results = jnp.stack(results, axis=0)
        updated[:, g * CHUNK : (g + 1) * CHUNK, :] = jnp.swapaxes(results, 0, 1).astype(BF16)
        for k in far_first:
            out_copy(g, k).start()
        source, place = out_views(me, g)
        copy = pltpu.make_async_copy(source, place, local_sem.at[1, g])
        copy.start()
        own.append(copy)

    for g in range(chunks):
        own[chunks + g].wait()
        for k in range(1, n):
            out_copy(g, k).wait()


def per_device(trials, sensors, readings, noises, lists, tiers):
    n, spaces = lax.axis_size("member"), lax.axis_size("space")
    members, patch, quantities = trials.shape
    obs_count = lists.shape[1]
    halo = 5 * obs_count // 2
    domains = patch // n
    chunks = domains // CHUNK
    lines = members * n
    width = -(-(domains + 2 * halo) // 256) * 256
    rows = -(-(members + 2) // 16) * 16
    vmem = pl.BlockSpec(memory_space=pltpu.VMEM)
    anywhere = pl.BlockSpec(memory_space=pl.ANY)
    full_rows = -(-(lines + 2) // 8) * 8
    dma = pltpu.SemaphoreType.DMA
    return pl.pallas_call(
        functools.partial(analyse_kernel, n, spaces, halo, obs_count),
        out_shape=jax.ShapeDtypeStruct((members, patch, quantities), BF16),
        in_specs=[anywhere] * 6,
        out_specs=vmem,
        scratch_shapes=[
            pltpu.VMEM((members, patch), BF16),
            pltpu.VMEM((patch,), BF16),
            pltpu.VMEM((patch,), BF16),
            pltpu.VMEM((domains, obs_count), jnp.int32),
            pltpu.VMEM((patch,), jnp.int32),
            dma((5,)),
            pltpu.VMEM((rows, patch), BF16),
            pltpu.VMEM((lines, domains, quantities), BF16),
            pltpu.VMEM((lines, domains, quantities), BF16),
            pltpu.VMEM((3, n, rows, patch), BF16),
            pltpu.VMEM((full_rows, 3 * patch), F32),
            pltpu.VMEM((lines, width), F32),
            pltpu.VMEM((width, 2 * LANES), BF16),
            pltpu.VMEM((domains, width), F32),
            pltpu.VMEM((domains, width), F32),
            pltpu.VMEM((domains, lines, LANES), F32),
            pltpu.VMEM((domains, LANES), F32),
            pltpu.VMEM((domains, lines, LANES), BF16),
            pltpu.VMEM((1, LANES), F32),
            pltpu.VMEM((n * spaces, 1, LANES), F32),
            dma((chunks, n)), dma((chunks, n)), dma((chunks, n)), dma((chunks, n)),
            dma((2, chunks)), dma((3,)), dma((3,)), dma((3, n)), dma((3, n)), dma((n * spaces,)), dma((n * spaces,)),
        ],
        compiler_params=pltpu.CompilerParams(
            collective_id=0, has_side_effects=True, vmem_limit_bytes=48 << 20
        ),
        name="analyse",
    )(trials, sensors, readings, noises, lists, tiers)


def solution(mesh):
    return jax.shard_map(
        per_device,
        mesh=mesh,
        in_specs=(
            P("member", ("region", "space"), None),
            P("member", ("region", "space")),
            P(("region", "space")),
            P(("region", "space")),
            P(("region", "space"), None),
            P(("region", "space")),
        ),
        out_specs=P("member", ("region", "space"), None),
        check_vma=False,
    )
```
